32 devices in a mesh: chol: 8 (over z, x), orb: 4 (over y, core).
Axes of the slice: x: 2, y: 2, z: 4, core: 2. Of those that a mesh axis runs over, the one named last changes fastest.
Arguments:
- b_vectors: bfloat16 [16, 6400, 6400], P('chol', 'orb'), as said below
- gamma_density: bfloat16 [16, 6400, 400], P('chol', 'orb'), may hold values from -2 to 2
Outputs:
- orbital_gradient: float32 [6400, 400], P('orb', 'chol')
The draws below stay inside these ranges and needn't reach their ends.
Inputs may be any that keep to these rules, and one draw needn't show every extreme that they name: Each b_vectors[Q] is a symmetric matrix.
All inputs are finite; a program needn't handle non-finite values.
Results may differ from the reference program's by a relative error of at most 0.0003.
Values may be sent and summed in bfloat16 or wider, within the bound.
A program may use at most 128 MiB of HBM per device.

```python
import math
import jax
import jax.numpy as jnp
from jax import lax

NMO = 6400
NOCC = 400
NVEC = 16


def draw_b_vectors(key, part):
    vector_keys = jax.random.split(key, NVEC)

    def single(subkey):
        sample = jax.random.normal(subkey, (NMO, NMO), jnp.float32)
        symmetric = (sample + sample.T) * 0.5 ** 0.5 / math.sqrt(NMO)
        return symmetric.astype(jnp.bfloat16)
    return lax.map(single, vector_keys)


def raised(values, own_key, source, target, blocks, factor):
    def block_of(dim):
        return (jnp.arange(values.shape[dim]) // (values.shape[dim] // blocks)).reshape((-1,) + (1,) * (values.ndim - 1 - dim))

    first = jax.random.permutation(own_key, blocks)[block_of(target)]
    other_side = (block_of(target) + blocks // 2) % blocks
    return jnp.where((block_of(source) == first) | (block_of(source) == other_side), factor * values, values)


def steps_of(own_key, extent, cuts, low, top_value):
    def one(dim, parts):
        draws = jax.random.uniform(jax.random.fold_in(jax.random.fold_in(own_key, 6), dim), (parts,), jnp.float32, low / len(cuts), top_value / len(cuts))
        return jnp.repeat(jnp.exp(draws), extent[dim] // parts).reshape((-1,) + (1,) * (len(extent) - dim - 1))

    loudness = one(*cuts[0])
    for cut in cuts[1:]:
        loudness = loudness * one(*cut)
    return loudness


def gaussian_with(key, dims, deviation, limit, pieces, heavy, dtype=jnp.bfloat16):
    array = deviation * jax.random.normal(key, dims, jnp.float32)
    if pieces:
        array = array * steps_of(key, dims, pieces, -0.22, 0.18)
    return jnp.clip(raised(array, jax.random.fold_in(key, 3), *heavy), -limit, limit).astype(dtype)


def setup_inputs(seed: int = 0) -> dict:
    streams_of = jax.random.split(jax.random.key(seed), 3)
    return {
        "b_vectors": draw_b_vectors(jax.random.fold_in(streams_of[2], 71), 0),
        "gamma_density": gaussian_with(streams_of[1], (NVEC, NMO, NOCC), NVEC ** -0.5, 2.0, ((0, 8), (1, 4)), (0, 2, 8, 2.0)),
    }


def reference(b_vectors, gamma_density):
    def accumulate(running, operands):
        b_piece, g_piece = operands
        return running + jnp.dot(b_piece, g_piece, preferred_element_type=jnp.float32), None

    lagrangian, _ = lax.scan(accumulate, jnp.zeros((NMO, NOCC), jnp.float32), (b_vectors, gamma_density))
    stride = NMO // NOCC
    occupied = lagrangian[::stride]
    return lagrangian.at[::stride].set(occupied - occupied.T)
```

```python
import functools

import jax
import jax.numpy as jnp
from jax import lax
from jax.experimental import pallas as pl
from jax.experimental.pallas import tpu as pltpu
from jax.sharding import PartitionSpec as P

LANES = 128
PAIR = 2
SUB = 8
LAGS = 1, 3, 5, 7, 9
MESH = pl.DeviceIdType.MESH
F32 = jnp.float32


def gathered(b_vectors, gamma_density):
    partial_sum = jnp.einsum(
        "qpr,qri->pi",
        b_vectors,
        lax.all_gather(gamma_density, "orb", axis=1, tiled=True),
        preferred_element_type=F32,
    )
    row_block = lax.psum_scatter(partial_sum, "chol", scatter_dimension=1, tiled=True)
    stride = b_vectors.shape[2] // gamma_density.shape[2]
    own_occupied = row_block[::stride]
    full_columns = lax.all_gather(own_occupied, "chol", axis=1, tiled=True)
    exchanged = lax.all_to_all(full_columns, "orb", split_axis=1, concat_axis=0, tiled=True)
    flipped = exchanged.T
    col_offset = lax.axis_index("chol") * row_block.shape[1]
    mirrored = lax.dynamic_slice_in_dim(flipped, col_offset, row_block.shape[1], 1)
    return row_block.at[::stride].set(own_occupied - mirrored)


FINE, COARSE, SPLIT, BASE = 65535.0, 32385.0, 256.0, 255.0


def packed_tiles(n):
    return n - n // 3 + 1


def packed(v):
    m = v.shape[0] // 3
    top = jnp.maximum(jnp.max(jnp.abs(v), axis=0), 1e-30)
    fine = FINE / top
    coarse = COARSE / top
    a = jnp.round(v[0:m] * fine)
    b = jnp.round(v[m:2 * m] * fine)
    c = jnp.round(v[2 * m:3 * m] * coarse)
    high = jnp.round(c * (1 / BASE))
    low = c - high * BASE
    rest = [v[3 * m:]] if v.shape[0] > 3 * m else []
    return jnp.concatenate([a * SPLIT + high, b * SPLIT + low, *rest, top[None]], axis=0)


def opened(w, rest):
    m = (w.shape[0] - 1 - rest) // 2
    top = w[2 * m + rest]
    fine = top * (1 / FINE)
    coarse = top * (1 / COARSE)
    first, second = w[0:m], w[m:2 * m]
    a = jnp.round(first * (1 / SPLIT))
    b = jnp.round(second * (1 / SPLIT))
    c = (first - a * SPLIT) * BASE + (second - b * SPLIT)
    tail = [w[2 * m:2 * m + rest]] if rest else []
    return jnp.concatenate([a * fine, b * fine, c * coarse, *tail], axis=0)


def kernel(nz, rows, cols, stride, ta,
           b_ref, g_ref, out_ref,
           bbuf, gt, cbuf, rc, s, ex1, ey1, ex2, ey2, rx1, ry1, rx2, ry2, own, z1r, z2s, z2r, f, ms, mr,
           bsem, csem, x1sem, y1sem, x2sem, y2sem, z1sem, z2sem, msem):
    c, o = lax.axis_index("chol"), lax.axis_index("orb")
    z, x = c // PAIR, lax.rem(c, PAIR)
    y, k = o // PAIR, lax.rem(o, PAIR)
    zl, zh = lax.rem(z, 2), z // 2
    nvec = b_ref.shape[0]
    nocc = g_ref.shape[1]
    hx = nocc // PAIR
    tiles = hx // SUB
    tb = tiles - ta
    half = PAIR * rows
    nch = s.shape[0]
    shift = half // LANES - nch
    tz = z1r.shape[2]
    zstep = cols // SUB
    zrows = tz * SUB

    core_id = (c, o + 1 - 2 * k)
    x_id = (c + 1 - 2 * x, o)
    y_id = (c, o + PAIR - 2 * PAIR * y)
    near_id = (c + PAIR - 2 * PAIR * zl, o)
    far_id = (c + 2 * PAIR - 4 * PAIR * zh, o)

    def fetches(j, side):
        quadrant = 1 - k if side == 0 else k
        slot = PAIR * lax.rem(j, 2) + side
        out = []
        for q in range(nvec):
            for yy in range(PAIR):
                lane = pl.multiple_of((yy * (half // LANES) + quadrant * shift + j) * LANES, LANES)
                out.append(pltpu.make_async_copy(
                    b_ref.at[q, :, pl.ds(lane, LANES)],
                    bbuf.at[slot, q * rows:(q + 1) * rows, yy * LANES:(yy + 1) * LANES],
                    bsem.at[slot, q * PAIR + yy]))
        return out

    def remote(src, dst, send, recv, target):
        return pltpu.make_async_remote_copy(
            src_ref=src, dst_ref=dst, send_sem=send, recv_sem=recv,
            device_id=target, device_id_type=MESH)

    def core_copy(j):
        return remote(cbuf.at[j], rc.at[j], csem.at[0, j], csem.at[1, j], core_id)

    def x1_copy(j):
        return remote(ex1.at[j], rx1.at[j], x1sem.at[0, j], x1sem.at[1, j], x_id)

    def y1_copy(j):
        return remote(ey1.at[j], ry1.at[j], y1sem.at[0, j], y1sem.at[1, j], y_id)

    def y2_copy(j):
        return remote(ey2.at[j], ry2.at[j], y2sem.at[0, j], y2sem.at[1, j], y_id)

    def x2_copy(j):
        return remote(ex2.at[j], rx2.at[j], x2sem.at[0, j], x2sem.at[1, j], x_id)

    def near_copy(j, h):
        first = (1 - zl + 2 * h) * zstep
        return remote(own.at[j, pl.ds(first, tz)], z1r.at[j, h], z1sem.at[0, j, h], z1sem.at[1, j, h], near_id)

    def far_copy(j):
        return remote(z2s.at[j, 1 - zh], z2r.at[j], z2sem.at[0, j], z2sem.at[1, j], far_id)

    for j in range(2):
        for side in range(2):
            for copy in fetches(j, side):
                copy.start()

    barrier = pltpu.get_barrier_semaphore()

    def greet(target):
        pl.semaphore_signal(barrier, inc=1, device_id=target, device_id_type=MESH)

    for target in (core_id, x_id, y_id, near_id, far_id):
        greet(target)

    for h in range(2):
        @pl.when(2 * o + h != c)
        def _():
            greet((2 * o + h, c // 2))

    col = lax.broadcasted_iota(jnp.int32, (nocc, nocc), 1)
    row = lax.broadcasted_iota(jnp.int32, (nocc, nocc), 0)
    origin = row
    for xx in range(PAIR):
        for zz in range(nz):
            start = xx * hx + zz * cols
            delta = (zz * PAIR + xx) * cols - start
            origin = jnp.where((row >= start) & (row < start + cols), row + delta, origin)
    pick = jnp.where(col == origin, 1.0, 0.0).astype(jnp.bfloat16)
    parts = [jnp.dot(pick, g_ref[q], preferred_element_type=F32) for q in range(nvec)]
    gt[...] = jnp.concatenate(parts, axis=1).astype(jnp.bfloat16)

    count = 5 + jnp.where(c // 2 == o, 1, 2)
    pl.semaphore_wait(barrier, count)

    def product(t, side):
        slot = PAIR * lax.rem(t, 2) + side
        for copy in fetches(t, side):
            copy.wait()
        dst = cbuf if side == 0 else s
        res = jnp.dot(gt[...], bbuf[slot], preferred_element_type=F32)
        for yy in range(PAIR):
            for xx in range(PAIR):
                part = res[xx * hx:(xx + 1) * hx, yy * LANES:(yy + 1) * LANES]
                dst[t, yy, xx] = part.reshape(tiles, SUB, LANES)

        @pl.when(t + 2 < nch)
        def _():
            for copy in fetches(t + 2, side):
                copy.start()

    def at_lag(t, lag, run):
        j = t - lag

        @pl.when((j >= 0) & (j < nch))
        def _():
            run(j)

    def between_cores(j):
        core_copy(j).wait_recv()
        away = [s[j, yy, 1 - x, 0:ta] + rc[j, yy, 1 - x, 0:ta] for yy in range(PAIR)]
        ex1[j] = packed(jnp.concatenate(away, axis=0))
        x1_copy(j).start()
        away = [s[j, 1 - y, xx, ta:tiles] + rc[j, 1 - y, xx, ta:tiles] for xx in range(PAIR)]
        ey1[j] = packed(jnp.concatenate(away, axis=0))
        y1_copy(j).start()
        for yy in range(PAIR):
            s[j, yy, x, 0:ta] = s[j, yy, x, 0:ta] + rc[j, yy, x, 0:ta]
        for xx in range(PAIR):
            s[j, y, xx, ta:tiles] = s[j, y, xx, ta:tiles] + rc[j, y, xx, ta:tiles]

    def first_done(j):
        x1_copy(j).wait_recv()
        arrived = opened(rx1[j], PAIR * ta % 3)
        s[j, 0, x, 0:ta] = s[j, 0, x, 0:ta] + arrived[0:ta]
        s[j, 1, x, 0:ta] = s[j, 1, x, 0:ta] + arrived[ta:2 * ta]
        ey2[j] = packed(s[j, 1 - y, x, 0:ta])
        y2_copy(j).start()
        y1_copy(j).wait_recv()
        arrived = opened(ry1[j], PAIR * tb % 3)
        s[j, y, 0, ta:tiles] = s[j, y, 0, ta:tiles] + arrived[0:tb]
        s[j, y, 1, ta:tiles] = s[j, y, 1, ta:tiles] + arrived[tb:2 * tb]
        ex2[j] = packed(s[j, y, 1 - x, ta:tiles])
        x2_copy(j).start()

    def second_done(j):
        y2_copy(j).wait_recv()
        own[j, 0:ta] = s[j, y, x, 0:ta] + opened(ry2[j], ta % 3)
        x2_copy(j).wait_recv()
        own[j, ta:tiles] = s[j, y, x, ta:tiles] + opened(rx2[j], tb % 3)
        for h in range(2):
            near_copy(j, h).start()

    def near_done(j):
        for h in range(2):
            near_copy(j, h).wait_recv()
            z2s[j, h] = own[j, pl.ds((zl + 2 * h) * zstep, tz)] + z1r[j, h]
        far_copy(j).start()

    def collect(j):
        far_copy(j).wait_recv()
        total = (z2s[j, zh] + z2r[j]).reshape(zrows, LANES)
        for h in range(nz):
            @pl.when(z == h)
            def _():
                lead = h * (cols - zstep * SUB)
                square = jnp.concatenate([total[lead:lead + cols], jnp.zeros((LANES - cols, LANES), F32)], axis=0)
                f[pl.ds(pl.multiple_of(j * LANES, LANES), LANES), :] = square.T

    def step(t, carry):
        @pl.when(t < nch)
        def _():
            product(t, 0)
            core_copy(t).start()

        at_lag(t, LAGS[0], between_cores)
        at_lag(t, LAGS[1], first_done)
        at_lag(t, LAGS[2], second_done)
        at_lag(t, LAGS[3], near_done)
        at_lag(t, LAGS[4], collect)

        @pl.when(t < nch)
        def _():
            product(t, 1)

        return carry

    lax.fori_loop(0, nch + LAGS[4], step, 0)

    off = k * (rows - shift * LANES)

    def mirror_copy(h, slot):
        return remote(ms.at[h], mr.at[slot], msem.at[0, h], msem.at[1, slot], (2 * o + h, c // 2))

    for h in range(2):
        block = f[pl.ds(off + h * stride * cols, cols, stride), :]
        ms[h] = jnp.concatenate([block, jnp.zeros((zrows - cols, LANES), F32)], axis=0)

        @pl.when(2 * o + h != c)
        def _():
            mirror_copy(h, x).start()

        @pl.when(2 * o + h == c)
        def _():
            mr[x] = ms[h]

    def drain(j, carry):
        for copy in (core_copy, x1_copy, y1_copy, x2_copy, y2_copy, far_copy):
            copy(j).wait_send()
        for h in range(2):
            near_copy(j, h).wait_send()
        return carry

    lax.fori_loop(0, nch, drain, 0)

    for h in range(2):
        @pl.when(2 * o + h != c)
        def _():
            mirror_copy(h, x).wait_send()
            mirror_copy(h, h).wait_recv()

    for h in range(2):
        square = jnp.concatenate([mr[h], jnp.zeros((LANES - zrows, LANES), F32)], axis=0).T
        where = pl.ds(off + h * stride * cols, cols, stride)
        f[where, :] = f[where, :] - square[0:cols]
    out_ref[...] = f[pl.ds(pl.multiple_of(off, 8), rows), 0:cols]


def mirrored_sums(nz, b_vectors, gamma_density):
    nvec, rows, nmo = b_vectors.shape
    nocc = gamma_density.shape[2]
    cols = nocc // (nz * PAIR)
    hx = nocc // PAIR
    tiles = hx // SUB
    ta = (tiles + 1) // 2
    tb = tiles - ta
    tz = pl.cdiv(cols, SUB)
    nch = pl.cdiv(rows, LANES)
    depth = nvec * rows
    vmem = pltpu.VMEM
    dma = pltpu.SemaphoreType.DMA
    flops = 2 * depth * nmo * nocc
    parts = [packed_tiles(n) for n in (PAIR * ta, PAIR * tb, tb, ta)]
    blocks = [vmem((nch, n, SUB, LANES), F32) for n in parts]
    return pl.pallas_call(
        functools.partial(kernel, nz, rows, cols, nmo // nocc, ta),
        out_shape=jax.ShapeDtypeStruct((rows, cols), F32),
        in_specs=[pl.BlockSpec(memory_space=pl.ANY), pl.BlockSpec(memory_space=vmem)],
        out_specs=pl.BlockSpec(memory_space=vmem),
        scratch_shapes=[
            vmem((2 * PAIR, depth, PAIR * LANES), jnp.bfloat16),
            vmem((nocc, depth), jnp.bfloat16),
            vmem((nch, PAIR, PAIR, tiles, SUB, LANES), F32),
            vmem((nch, PAIR, PAIR, tiles, SUB, LANES), F32),
            vmem((nch, PAIR, PAIR, tiles, SUB, LANES), F32),
            *blocks,
            *blocks,
            vmem((nch, tiles, SUB, LANES), F32),
            vmem((nch, 2, tz, SUB, LANES), F32),
            vmem((nch, 2, tz, SUB, LANES), F32),
            vmem((nch, tz, SUB, LANES), F32),
            vmem((nch * LANES, LANES), F32),
            vmem((2, tz * SUB, LANES), F32),
            vmem((2, tz * SUB, LANES), F32),
            dma((2 * PAIR, nvec * PAIR)),
            dma((2, nch)),
            dma((2, nch)),
            dma((2, nch)),
            dma((2, nch)),
            dma((2, nch)),
            dma((2, nch, 2)),
            dma((2, nch)),
            dma((2, 2)),
        ],
        compiler_params=pltpu.CompilerParams(
            collective_id=0, has_side_effects=True, vmem_limit_bytes=60 * 2**20
        ),
        cost_estimate=pl.CostEstimate(flops=flops, bytes_accessed=2 * depth * nmo, transcendentals=0),
    )(b_vectors, jnp.transpose(gamma_density, (0, 2, 1)))


def solution(mesh):
    nchol, norb = mesh.shape["chol"], mesh.shape["orb"]

    def shards(b_vectors, gamma_density):
        nvec, rows, nmo = b_vectors.shape
        nocc = gamma_density.shape[2]
        cols = nocc // nchol
        fits = (
            norb == PAIR * PAIR
            and nchol == PAIR * norb
            and (PAIR * rows) % LANES == 0
            and rows % 16 == 0
            and nocc % (PAIR * nchol) == 0
            and (nocc // PAIR) % SUB == 0
            and nchol == 8
            and cols % SUB * (nchol // PAIR) <= SUB
            and (nvec * rows) % LANES == 0
            and nmo % nocc == 0
            and rows % (nmo // nocc) == 0
        )
        if fits:
            return mirrored_sums(nchol // PAIR, b_vectors, gamma_density)
        return gathered(b_vectors, gamma_density)

    in_specs = (P("chol", "orb", None), P("chol", "orb", None))
    out_specs = P("orb", "chol")
    return jax.shard_map(shards, mesh=mesh, in_specs=in_specs, out_specs=out_specs, check_vma=False)
```

```python
import functools

import jax
import jax.numpy as jnp
from jax import lax
from jax.experimental import pallas as pl
from jax.experimental.pallas import tpu as pltpu
from jax.sharding import PartitionSpec as P

LANES = 128
PAIR = 2
SUB = 8
LAGS = 1, 4, 7, 10, 13
MESH = pl.DeviceIdType.MESH
F32 = jnp.float32


def gathered(b_vectors, gamma_density):
    partial_sum = jnp.einsum(
        "qpr,qri->pi",
        b_vectors,
        lax.all_gather(gamma_density, "orb", axis=1, tiled=True),
        preferred_element_type=F32,
    )
    row_block = lax.psum_scatter(partial_sum, "chol", scatter_dimension=1, tiled=True)
    stride = b_vectors.shape[2] // gamma_density.shape[2]
    own_occupied = row_block[::stride]
    full_columns = lax.all_gather(own_occupied, "chol", axis=1, tiled=True)
    exchanged = lax.all_to_all(full_columns, "orb", split_axis=1, concat_axis=0, tiled=True)
    flipped = exchanged.T
    col_offset = lax.axis_index("chol") * row_block.shape[1]
    mirrored = lax.dynamic_slice_in_dim(flipped, col_offset, row_block.shape[1], 1)
    return row_block.at[::stride].set(own_occupied - mirrored)


FINE, COARSE, SPLIT, BASE = 65535.0, 32385.0, 256.0, 255.0
EVEN, SLOT, STEP, NINE = 8187.0, 2048.0, 8.0, 9.0


def grouping(n):
    sevens, left = divmod(n, 7)
    threes, rest = divmod(left, 3)
    return sevens, threes, rest


def packed_tiles(n):
    sevens, threes, rest = grouping(n)
    return 4 * sevens + 2 * threes + rest + 1


def packed(v):
    m, t, rest = grouping(v.shape[0])
    top = jnp.maximum(jnp.max(jnp.abs(v), axis=0), 1e-30)
    words = []
    if m:
        even = EVEN / top
        q = [jnp.round(v[i * m:(i + 1) * m] * even) for i in range(7)]
        high = [jnp.round(e * (1 / STEP)) for e in q[4:]]
        low = [e - h * STEP for e, h in zip(q[4:], high)]
        high.append((low[0] * NINE + low[1]) * NINE + low[2])
        words += [a * SLOT + h for a, h in zip(q[:4], high)]
    if t:
        u = v[7 * m:7 * m + 3 * t]
        fine, coarse = FINE / top, COARSE / top
        a, b, c = jnp.round(u[0:t] * fine), jnp.round(u[t:2 * t] * fine), jnp.round(u[2 * t:3 * t] * coarse)
        high = jnp.round(c * (1 / BASE))
        words += [a * SPLIT + high, b * SPLIT + (c - high * BASE)]
    if rest:
        words.append(v[7 * m + 3 * t:])
    return jnp.concatenate([*words, top[None]], axis=0)


def opened(w, n):
    m, t, rest = grouping(n)
    top = w[w.shape[0] - 1]
    values = []
    if m:
        even = top * (1 / EVEN)
        first = [w[i * m:(i + 1) * m] for i in range(4)]
        whole = [jnp.round(e * (1 / SLOT)) for e in first]
        slot = [e - a * SLOT for e, a in zip(first, whole)]
        low0 = jnp.round(slot[3] * (1 / (NINE * NINE)))
        left = slot[3] - low0 * (NINE * NINE)
        low1 = jnp.round(left * (1 / NINE))
        low = [low0, low1, left - low1 * NINE]
        whole += [h * STEP + e for h, e in zip(slot[:3], low)]
        values += [a * even for a in whole]
    if t:
        fine, coarse = top * (1 / FINE), top * (1 / COARSE)
        first, second = w[4 * m:4 * m + t], w[4 * m + t:4 * m + 2 * t]
        a, b = jnp.round(first * (1 / SPLIT)), jnp.round(second * (1 / SPLIT))
        c = (first - a * SPLIT) * BASE + (second - b * SPLIT)
        values += [a * fine, b * fine, c * coarse]
    if rest:
        values.append(w[4 * m + 2 * t:4 * m + 2 * t + rest])
    return jnp.concatenate(values, axis=0)


def kernel(nz, rows, cols, stride, ta,
           b_ref, g_ref, out_ref,
           bbuf, gbuf, gt, cbuf, rc, s, ex1, ey1, ex2, ey2, rx1, ry1, rx2, ry2, own, z1r, z2s, z2r, f, ms, mr,
           bsem, gsem, csem, x1sem, y1sem, x2sem, y2sem, z1sem, z2sem, msem):
    c, o = lax.axis_index("chol"), lax.axis_index("orb")
    z, x = c // PAIR, lax.rem(c, PAIR)
    y, k = o // PAIR, lax.rem(o, PAIR)
    zl, zh = lax.rem(z, 2), z // 2
    nvec = b_ref.shape[0]
    nocc = g_ref.shape[1]
    hx = nocc // PAIR
    tiles = hx // SUB
    tb = tiles - ta
    half = PAIR * rows
    nch = s.shape[0]
    shift = half // LANES - nch
    tz = z1r.shape[2]
    zstep = cols // SUB
    zrows = tz * SUB

    core_id = (c, o + 1 - 2 * k)
    x_id = (c + 1 - 2 * x, o)
    y_id = (c, o + PAIR - 2 * PAIR * y)
    near_id = (c + PAIR - 2 * PAIR * zl, o)
    far_id = (c + 2 * PAIR - 4 * PAIR * zh, o)

    def fetches(j, side):
        quadrant = 1 - k if side == 0 else k
        slot = PAIR * lax.rem(j, 2) + side
        out = []
        for q in range(nvec):
            for yy in range(PAIR):
                lane = pl.multiple_of((yy * (half // LANES) + quadrant * shift + j) * LANES, LANES)
                out.append(pltpu.make_async_copy(
                    b_ref.at[q, :, pl.ds(lane, LANES)],
                    bbuf.at[slot, q * rows:(q + 1) * rows, yy * LANES:(yy + 1) * LANES],
                    bsem.at[slot, q * PAIR + yy]))
        return out

    def remote(src, dst, send, recv, target):
        return pltpu.make_async_remote_copy(
            src_ref=src, dst_ref=dst, send_sem=send, recv_sem=recv,
            device_id=target, device_id_type=MESH)

    def core_copy(j):
        return remote(cbuf.at[j], rc.at[j], csem.at[0, j], csem.at[1, j], core_id)

    def x1_copy(j):
        return remote(ex1.at[j], rx1.at[j], x1sem.at[0, j], x1sem.at[1, j], x_id)

    def y1_copy(j):
        return remote(ey1.at[j], ry1.at[j], y1sem.at[0, j], y1sem.at[1, j], y_id)

    def y2_copy(j):
        return remote(ey2.at[j], ry2.at[j], y2sem.at[0, j], y2sem.at[1, j], y_id)

    def x2_copy(j):
        return remote(ex2.at[j], rx2.at[j], x2sem.at[0, j], x2sem.at[1, j], x_id)

    def near_copy(j, h):
        first = (1 - zl + 2 * h) * zstep
        return remote(own.at[j, pl.ds(first, tz)], z1r.at[j, h], z1sem.at[0, j, h], z1sem.at[1, j, h], near_id)

    def far_copy(j):
        return remote(z2s.at[j, 1 - zh], z2r.at[j], z2sem.at[0, j], z2sem.at[1, j], far_id)

    loads = [pltpu.make_async_copy(g_ref.at[q], gbuf.at[q], gsem.at[q]) for q in range(nvec)]
    for copy in loads:
        copy.start()
    for j in range(2):
        for side in range(2):
            for copy in fetches(j, side):
                copy.start()

    barrier = pltpu.get_barrier_semaphore()

    def greet(target):
        pl.semaphore_signal(barrier, inc=1, device_id=target, device_id_type=MESH)

    for target in (core_id, x_id, y_id, near_id, far_id):
        greet(target)

    for h in range(2):
        @pl.when(2 * o + h != c)
        def _():
            greet((2 * o + h, c // 2))

    col = lax.broadcasted_iota(jnp.int32, (nocc, nocc), 1)
    row = lax.broadcasted_iota(jnp.int32, (nocc, 1), 0)
    origin = row
    for xx in range(PAIR):
        for zz in range(nz):
            start = xx * hx + zz * cols
            delta = (zz * PAIR + xx) * cols - start
            origin = jnp.where((row >= start) & (row < start + cols), row + delta, origin)
    pick = jnp.where(col == origin, 1.0, 0.0).astype(jnp.bfloat16)
    parts = []
    for q in range(nvec):
        loads[q].wait()
        parts.append(jnp.dot(pick, gbuf[q], preferred_element_type=F32))
    gt[...] = jnp.concatenate(parts, axis=1).astype(jnp.bfloat16)

    count = 5 + jnp.where(c // 2 == o, 1, 2)
    pl.semaphore_wait(barrier, count)

    def product(t, side):
        slot = PAIR * lax.rem(t, 2) + side
        for copy in fetches(t, side):
            copy.wait()
        dst = cbuf if side == 0 else s
        res = jnp.dot(gt[...], bbuf[slot], preferred_element_type=F32)
        for yy in range(PAIR):
            for xx in range(PAIR):
                part = res[xx * hx:(xx + 1) * hx, yy * LANES:(yy + 1) * LANES]
                dst[t, yy, xx] = part.reshape(tiles, SUB, LANES)

        @pl.when(t + 2 < nch)
        def _():
            for copy in fetches(t + 2, side):
                copy.start()

    def at_lag(t, lag, run):
        j = t - lag

        @pl.when((j >= 0) & (j < nch))
        def _():
            run(j)

    def between_cores(j):
        core_copy(j).wait_recv()
        away = [s[j, yy, 1 - x, 0:ta] + rc[j, yy, 1 - x, 0:ta] for yy in range(PAIR)]
        ex1[j] = packed(jnp.concatenate(away, axis=0))
        x1_copy(j).start()
        away = [s[j, 1 - y, xx, ta:tiles] + rc[j, 1 - y, xx, ta:tiles] for xx in range(PAIR)]
        ey1[j] = packed(jnp.concatenate(away, axis=0))
        y1_copy(j).start()
        for yy in range(PAIR):
            s[j, yy, x, 0:ta] = s[j, yy, x, 0:ta] + rc[j, yy, x, 0:ta]
        for xx in range(PAIR):
            s[j, y, xx, ta:tiles] = s[j, y, xx, ta:tiles] + rc[j, y, xx, ta:tiles]

    def first_done(j):
        x1_copy(j).wait_recv()
        arrived = opened(rx1[j], PAIR * ta)
        s[j, 0, x, 0:ta] = s[j, 0, x, 0:ta] + arrived[0:ta]
        s[j, 1, x, 0:ta] = s[j, 1, x, 0:ta] + arrived[ta:2 * ta]
        ey2[j] = packed(s[j, 1 - y, x, 0:ta])
        y2_copy(j).start()
        y1_copy(j).wait_recv()
        arrived = opened(ry1[j], PAIR * tb)
        s[j, y, 0, ta:tiles] = s[j, y, 0, ta:tiles] + arrived[0:tb]
        s[j, y, 1, ta:tiles] = s[j, y, 1, ta:tiles] + arrived[tb:2 * tb]
        ex2[j] = packed(s[j, y, 1 - x, ta:tiles])
        x2_copy(j).start()

    def second_done(j):
        y2_copy(j).wait_recv()
        own[j, 0:ta] = s[j, y, x, 0:ta] + opened(ry2[j], ta)
        x2_copy(j).wait_recv()
        own[j, ta:tiles] = s[j, y, x, ta:tiles] + opened(rx2[j], tb)
        for h in range(2):
            near_copy(j, h).start()

    def near_done(j):
        for h in range(2):
            near_copy(j, h).wait_recv()
            z2s[j, h] = own[j, pl.ds((zl + 2 * h) * zstep, tz)] + z1r[j, h]
        far_copy(j).start()

    def collect(j):
        far_copy(j).wait_recv()
        total = (z2s[j, zh] + z2r[j]).reshape(zrows, LANES)
        for h in range(nz):
            @pl.when(z == h)
            def _():
                lead = h * (cols - zstep * SUB)
                square = jnp.concatenate([total[lead:lead + cols], jnp.zeros((LANES - cols, LANES), F32)], axis=0)
                f[pl.ds(pl.multiple_of(j * LANES, LANES), LANES), :] = square.T

    def step(t, carry):
        @pl.when(t < nch)
        def _():
            product(t, 0)
            core_copy(t).start()

        at_lag(t, LAGS[0], between_cores)
        at_lag(t, LAGS[1], first_done)
        at_lag(t, LAGS[2], second_done)
        at_lag(t, LAGS[3], near_done)
        at_lag(t, LAGS[4], collect)

        @pl.when(t < nch)
        def _():
            product(t, 1)

        return carry

    lax.fori_loop(0, nch + LAGS[4], step, 0)

    off = k * (rows - shift * LANES)

    def mirror_copy(h, slot):
        return remote(ms.at[h], mr.at[slot], msem.at[0, h], msem.at[1, slot], (2 * o + h, c // 2))

    for h in range(2):
        block = f[pl.ds(off + h * stride * cols, cols, stride), :]
        ms[h] = jnp.concatenate([block, jnp.zeros((zrows - cols, LANES), F32)], axis=0)

        @pl.when(2 * o + h != c)
        def _():
            mirror_copy(h, x).start()

        @pl.when(2 * o + h == c)
        def _():
            mr[x] = ms[h]

    def drain(j, carry):
        for copy in (core_copy, x1_copy, y1_copy, x2_copy, y2_copy, far_copy):
            copy(j).wait_send()
        for h in range(2):
            near_copy(j, h).wait_send()
        return carry

    lax.fori_loop(0, nch, drain, 0)

    for h in range(2):
        @pl.when(2 * o + h != c)
        def _():
            mirror_copy(h, x).wait_send()
            mirror_copy(h, h).wait_recv()

    for h in range(2):
        square = jnp.concatenate([mr[h], jnp.zeros((LANES - zrows, LANES), F32)], axis=0).T
        where = pl.ds(off + h * stride * cols, cols, stride)
        f[where, :] = f[where, :] - square[0:cols]
    out_ref[...] = f[pl.ds(pl.multiple_of(off, 8), rows), 0:cols]


def mirrored_sums(nz, b_vectors, gamma_density):
    nvec, rows, nmo = b_vectors.shape
    nocc = gamma_density.shape[2]
    cols = nocc // (nz * PAIR)
    hx = nocc // PAIR
    tiles = hx // SUB
    ta = min(tiles, (tiles // 2 + 6) // 7 * 7)
    tb = tiles - ta
    tz = pl.cdiv(cols, SUB)
    nch = pl.cdiv(rows, LANES)
    depth = nvec * rows
    vmem = pltpu.VMEM
    dma = pltpu.SemaphoreType.DMA
    flops = 2 * depth * nmo * nocc
    parts = [packed_tiles(n) for n in (PAIR * ta, PAIR * tb, tb, ta)]
    blocks = [vmem((nch, n, SUB, LANES), F32) for n in parts]
    return pl.pallas_call(
        functools.partial(kernel, nz, rows, cols, nmo // nocc, ta),
        out_shape=jax.ShapeDtypeStruct((rows, cols), F32),
        in_specs=[pl.BlockSpec(memory_space=pl.ANY), pl.BlockSpec(memory_space=pl.ANY)],
        out_specs=pl.BlockSpec(memory_space=vmem),
        scratch_shapes=[
            vmem((2 * PAIR, depth, PAIR * LANES), jnp.bfloat16),
            vmem((nvec, nocc, rows), jnp.bfloat16),
            vmem((nocc, depth), jnp.bfloat16),
            vmem((nch, PAIR, PAIR, tiles, SUB, LANES), F32),
            vmem((nch, PAIR, PAIR, tiles, SUB, LANES), F32),
            vmem((nch, PAIR, PAIR, tiles, SUB, LANES), F32),
            *blocks,
            *blocks,
            vmem((nch, tiles, SUB, LANES), F32),
            vmem((nch, 2, tz, SUB, LANES), F32),
            vmem((nch, 2, tz, SUB, LANES), F32),
            vmem((nch, tz, SUB, LANES), F32),
            vmem((nch * LANES, LANES), F32),
            vmem((2, tz * SUB, LANES), F32),
            vmem((2, tz * SUB, LANES), F32),
            dma((2 * PAIR, nvec * PAIR)),
            dma((nvec,)),
            dma((2, nch)),
            dma((2, nch)),
            dma((2, nch)),
            dma((2, nch)),
            dma((2, nch)),
            dma((2, nch, 2)),
            dma((2, nch)),
            dma((2, 2)),
        ],
        compiler_params=pltpu.CompilerParams(
            collective_id=0, has_side_effects=True, vmem_limit_bytes=60 * 2**20
        ),
        cost_estimate=pl.CostEstimate(flops=flops, bytes_accessed=2 * depth * nmo, transcendentals=0),
    )(b_vectors, jnp.transpose(gamma_density, (0, 2, 1)))


def solution(mesh):
    nchol, norb = mesh.shape["chol"], mesh.shape["orb"]

    def shards(b_vectors, gamma_density):
        nvec, rows, nmo = b_vectors.shape
        nocc = gamma_density.shape[2]
        cols = nocc // nchol
        fits = (
            norb == PAIR * PAIR
            and nchol == PAIR * norb
            and (PAIR * rows) % LANES == 0
            and rows % 16 == 0
            and nocc % (PAIR * nchol) == 0
            and (nocc // PAIR) % SUB == 0
            and nchol == 8
            and cols % SUB * (nchol // PAIR) <= SUB
            and (nvec * rows) % LANES == 0
            and nmo % nocc == 0
            and rows % (nmo // nocc) == 0
        )
        if fits:
            return mirrored_sums(nchol // PAIR, b_vectors, gamma_density)
        return gathered(b_vectors, gamma_density)

    in_specs = (P("chol", "orb", None), P("chol", "orb", None))
    out_specs = P("orb", "chol")
    return jax.shard_map(shards, mesh=mesh, in_specs=in_specs, out_specs=out_specs, check_vma=False)
```

```python
import functools

import jax
import jax.numpy as jnp
from jax import lax
from jax.experimental import pallas as pl
from jax.experimental.pallas import tpu as pltpu
from jax.sharding import PartitionSpec as P

LANES = 128
PAIR = 2
SUB = 8
LAGS = 1, 3, 5, 7, 9
MESH = pl.DeviceIdType.MESH
F32 = jnp.float32


def gathered(b_vectors, gamma_density):
    partial_sum = jnp.einsum(
        "qpr,qri->pi",
        b_vectors,
        lax.all_gather(gamma_density, "orb", axis=1, tiled=True),
        preferred_element_type=F32,
    )
    row_block = lax.psum_scatter(partial_sum, "chol", scatter_dimension=1, tiled=True)
    stride = b_vectors.shape[2] // gamma_density.shape[2]
    own_occupied = row_block[::stride]
    full_columns = lax.all_gather(own_occupied, "chol", axis=1, tiled=True)
    exchanged = lax.all_to_all(full_columns, "orb", split_axis=1, concat_axis=0, tiled=True)
    flipped = exchanged.T
    col_offset = lax.axis_index("chol") * row_block.shape[1]
    mirrored = lax.dynamic_slice_in_dim(flipped, col_offset, row_block.shape[1], 1)
    return row_block.at[::stride].set(own_occupied - mirrored)


FINE, COARSE, SPLIT, BASE = 65535.0, 32385.0, 256.0, 255.0
EVEN, SLOT, STEP, NINE = 8187.0, 2048.0, 8.0, 9.0


def grouping(n):
    sevens, left = divmod(n, 7)
    threes, rest = divmod(left, 3)
    return sevens, threes, rest


def packed_tiles(n):
    sevens, threes, rest = grouping(n)
    return 4 * sevens + 2 * threes + rest + 1


def packed(v):
    m, t, rest = grouping(v.shape[0])
    top = jnp.maximum(jnp.max(jnp.abs(v), axis=0), 1e-30)
    words = []
    if m:
        even = EVEN / top
        q = [jnp.round(v[i * m:(i + 1) * m] * even) for i in range(7)]
        high = [jnp.round(e * (1 / STEP)) for e in q[4:]]
        low = [e - h * STEP for e, h in zip(q[4:], high)]
        high.append((low[0] * NINE + low[1]) * NINE + low[2])
        words += [a * SLOT + h for a, h in zip(q[:4], high)]
    if t:
        u = v[7 * m:7 * m + 3 * t]
        fine, coarse = FINE / top, COARSE / top
        a, b, c = jnp.round(u[0:t] * fine), jnp.round(u[t:2 * t] * fine), jnp.round(u[2 * t:3 * t] * coarse)
        high = jnp.round(c * (1 / BASE))
        words += [a * SPLIT + high, b * SPLIT + (c - high * BASE)]
    if rest:
        words.append(v[7 * m + 3 * t:])
    return jnp.concatenate([*words, top[None]], axis=0)


def opened(w, n):
    m, t, rest = grouping(n)
    top = w[w.shape[0] - 1]
    values = []
    if m:
        even = top * (1 / EVEN)
        first = [w[i * m:(i + 1) * m] for i in range(4)]
        whole = [jnp.round(e * (1 / SLOT)) for e in first]
        slot = [e - a * SLOT for e, a in zip(first, whole)]
        low0 = jnp.round(slot[3] * (1 / (NINE * NINE)))
        left = slot[3] - low0 * (NINE * NINE)
        low1 = jnp.round(left * (1 / NINE))
        low = [low0, low1, left - low1 * NINE]
        whole += [h * STEP + e for h, e in zip(slot[:3], low)]
        values += [a * even for a in whole]
    if t:
        fine, coarse = top * (1 / FINE), top * (1 / COARSE)
        first, second = w[4 * m:4 * m + t], w[4 * m + t:4 * m + 2 * t]
        a, b = jnp.round(first * (1 / SPLIT)), jnp.round(second * (1 / SPLIT))
        c = (first - a * SPLIT) * BASE + (second - b * SPLIT)
        values += [a * fine, b * fine, c * coarse]
    if rest:
        values.append(w[4 * m + 2 * t:4 * m + 2 * t + rest])
    return jnp.concatenate(values, axis=0)


def kernel(nz, rows, cols, stride, ta,
           b_ref, g_ref, out_ref,
           bbuf, gbuf, gt, cbuf, rc, s, ex1, ey1, ex2, ey2, rx1, ry1, rx2, ry2, own, z1r, z2s, z2r, f, ms, mr,
           bsem, gsem, csem, x1sem, y1sem, x2sem, y2sem, z1sem, z2sem, msem):
    c, o = lax.axis_index("chol"), lax.axis_index("orb")
    z, x = c // PAIR, lax.rem(c, PAIR)
    y, k = o // PAIR, lax.rem(o, PAIR)
    zl, zh = lax.rem(z, 2), z // 2
    nvec = b_ref.shape[0]
    nocc = g_ref.shape[1]
    hx = nocc // PAIR
    tiles = hx // SUB
    tb = tiles - ta
    half = PAIR * rows
    nch = s.shape[0]
    shift = half // LANES - nch
    tz = z1r.shape[2]
    zstep = cols // SUB
    zrows = tz * SUB

    core_id = (c, o + 1 - 2 * k)
    x_id = (c + 1 - 2 * x, o)
    y_id = (c, o + PAIR - 2 * PAIR * y)
    near_id = (c + PAIR - 2 * PAIR * zl, o)
    far_id = (c + 2 * PAIR - 4 * PAIR * zh, o)

    def fetches(j, side):
        quadrant = 1 - k if side == 0 else k
        slot = PAIR * lax.rem(j, 2) + side
        out = []
        for q in range(nvec):
            for yy in range(PAIR):
                lane = pl.multiple_of((yy * (half // LANES) + quadrant * shift + j) * LANES, LANES)
                out.append(pltpu.make_async_copy(
                    b_ref.at[q, :, pl.ds(lane, LANES)],
                    bbuf.at[slot, q * rows:(q + 1) * rows, yy * LANES:(yy + 1) * LANES],
                    bsem.at[slot, q * PAIR + yy]))
        return out

    def remote(src, dst, send, recv, target):
        return pltpu.make_async_remote_copy(
            src_ref=src, dst_ref=dst, send_sem=send, recv_sem=recv,
            device_id=target, device_id_type=MESH)

    def core_copy(j):
        return remote(cbuf.at[j], rc.at[j], csem.at[0, j], csem.at[1, j], core_id)

    def x1_copy(j):
        return remote(ex1.at[j], rx1.at[j], x1sem.at[0, j], x1sem.at[1, j], x_id)

    def y1_copy(j):
        return remote(ey1.at[j], ry1.at[j], y1sem.at[0, j], y1sem.at[1, j], y_id)

    def y2_copy(j):
        return remote(ey2.at[j], ry2.at[j], y2sem.at[0, j], y2sem.at[1, j], y_id)

    def x2_copy(j):
        return remote(ex2.at[j], rx2.at[j], x2sem.at[0, j], x2sem.at[1, j], x_id)

    def near_copy(j, h):
        first = (1 - zl + 2 * h) * zstep
        return remote(own.at[j, pl.ds(first, tz)], z1r.at[j, h], z1sem.at[0, j, h], z1sem.at[1, j, h], near_id)

    def far_copy(j):
        return remote(z2s.at[j, 1 - zh], z2r.at[j], z2sem.at[0, j], z2sem.at[1, j], far_id)

    loads = [pltpu.make_async_copy(g_ref.at[q], gbuf.at[q], gsem.at[q]) for q in range(nvec)]
    for copy in loads:
        copy.start()
    for j in range(2):
        for side in range(2):
            for copy in fetches(j, side):
                copy.start()

    barrier = pltpu.get_barrier_semaphore()

    def greet(target):
        pl.semaphore_signal(barrier, inc=1, device_id=target, device_id_type=MESH)

    for target in (core_id, x_id, y_id, near_id, far_id):
        greet(target)

    for h in range(2):
        @pl.when(2 * o + h != c)
        def _():
            greet((2 * o + h, c // 2))

    col = lax.broadcasted_iota(jnp.int32, (nocc, nocc), 1)
    row = lax.broadcasted_iota(jnp.int32, (nocc, 1), 0)
    origin = row
    for xx in range(PAIR):
        for zz in range(nz):
            start = xx * hx + zz * cols
            delta = (zz * PAIR + xx) * cols - start
            origin = jnp.where((row >= start) & (row < start + cols), row + delta, origin)
    pick = jnp.where(col == origin, 1.0, 0.0).astype(jnp.bfloat16)
    parts = []
    for q in range(nvec):
        loads[q].wait()
        parts.append(jnp.dot(pick, gbuf[q], preferred_element_type=F32))
    gt[...] = jnp.concatenate(parts, axis=1).astype(jnp.bfloat16)

    count = 5 + jnp.where(c // 2 == o, 1, 2)
    pl.semaphore_wait(barrier, count)

    def product(t, side):
        slot = PAIR * lax.rem(t, 2) + side
        for copy in fetches(t, side):
            copy.wait()
        dst = cbuf if side == 0 else s
        res = jnp.dot(gt[...], bbuf[slot], preferred_element_type=F32)
        for yy in range(PAIR):
            for xx in range(PAIR):
                part = res[xx * hx:(xx + 1) * hx, yy * LANES:(yy + 1) * LANES]
                dst[t, yy, xx] = part.reshape(tiles, SUB, LANES)

        @pl.when(t + 2 < nch)
        def _():
            for copy in fetches(t + 2, side):
                copy.start()

    def at_lag(t, lag, run):
        j = t - lag

        @pl.when((j >= 0) & (j < nch))
        def _():
            run(j)

    def between_cores(j):
        core_copy(j).wait_recv()
        away = [s[j, yy, 1 - x, 0:ta] + rc[j, yy, 1 - x, 0:ta] for yy in range(PAIR)]
        ex1[j] = packed(jnp.concatenate(away, axis=0))
        x1_copy(j).start()
        away = [s[j, 1 - y, xx, ta:tiles] + rc[j, 1 - y, xx, ta:tiles] for xx in range(PAIR)]
        ey1[j] = packed(jnp.concatenate(away, axis=0))
        y1_copy(j).start()
        for yy in range(PAIR):
            s[j, yy, x, 0:ta] = s[j, yy, x, 0:ta] + rc[j, yy, x, 0:ta]
        for xx in range(PAIR):
            s[j, y, xx, ta:tiles] = s[j, y, xx, ta:tiles] + rc[j, y, xx, ta:tiles]

    def first_done(j):
        x1_copy(j).wait_recv()
        arrived = opened(rx1[j], PAIR * ta)
        s[j, 0, x, 0:ta] = s[j, 0, x, 0:ta] + arrived[0:ta]
        s[j, 1, x, 0:ta] = s[j, 1, x, 0:ta] + arrived[ta:2 * ta]
        ey2[j] = packed(s[j, 1 - y, x, 0:ta])
        y2_copy(j).start()
        y1_copy(j).wait_recv()
        arrived = opened(ry1[j], PAIR * tb)
        s[j, y, 0, ta:tiles] = s[j, y, 0, ta:tiles] + arrived[0:tb]
        s[j, y, 1, ta:tiles] = s[j, y, 1, ta:tiles] + arrived[tb:2 * tb]
        ex2[j] = packed(s[j, y, 1 - x, ta:tiles])
        x2_copy(j).start()

    def second_done(j):
        y2_copy(j).wait_recv()
        own[j, 0:ta] = s[j, y, x, 0:ta] + opened(ry2[j], ta)
        x2_copy(j).wait_recv()
        own[j, ta:tiles] = s[j, y, x, ta:tiles] + opened(rx2[j], tb)
        for h in range(2):
            near_copy(j, h).start()

    def near_done(j):
        for h in range(2):
            near_copy(j, h).wait_recv()
            z2s[j, h] = own[j, pl.ds((zl + 2 * h) * zstep, tz)] + z1r[j, h]
        far_copy(j).start()

    def collect(j):
        far_copy(j).wait_recv()
        total = (z2s[j, zh] + z2r[j]).reshape(zrows, LANES)
        for h in range(nz):
            @pl.when(z == h)
            def _():
                lead = h * (cols - zstep * SUB)
                square = jnp.concatenate([total[lead:lead + cols], jnp.zeros((LANES - cols, LANES), F32)], axis=0)
                f[pl.ds(pl.multiple_of(j * LANES, LANES), LANES), :] = square.T

    def step(t, carry):
        @pl.when(t < nch)
        def _():
            product(t, 0)
            core_copy(t).start()

        at_lag(t, LAGS[0], between_cores)
        at_lag(t, LAGS[1], first_done)
        at_lag(t, LAGS[2], second_done)
        at_lag(t, LAGS[3], near_done)
        at_lag(t, LAGS[4], collect)

        @pl.when(t < nch)
        def _():
            product(t, 1)

        return carry

    lax.fori_loop(0, nch + LAGS[4], step, 0)

    off = k * (rows - shift * LANES)

    def mirror_copy(h, slot):
        return remote(ms.at[h], mr.at[slot], msem.at[0, h], msem.at[1, slot], (2 * o + h, c // 2))

    for h in range(2):
        block = f[pl.ds(off + h * stride * cols, cols, stride), :]
        ms[h] = jnp.concatenate([block, jnp.zeros((zrows - cols, LANES), F32)], axis=0)

        @pl.when(2 * o + h != c)
        def _():
            mirror_copy(h, x).start()

        @pl.when(2 * o + h == c)
        def _():
            mr[x] = ms[h]

    def drain(j, carry):
        for copy in (core_copy, x1_copy, y1_copy, x2_copy, y2_copy, far_copy):
            copy(j).wait_send()
        for h in range(2):
            near_copy(j, h).wait_send()
        return carry

    lax.fori_loop(0, nch, drain, 0)

    for h in range(2):
        @pl.when(2 * o + h != c)
        def _():
            mirror_copy(h, x).wait_send()
            mirror_copy(h, h).wait_recv()

    for h in range(2):
        square = jnp.concatenate([mr[h], jnp.zeros((LANES - zrows, LANES), F32)], axis=0).T
        where = pl.ds(off + h * stride * cols, cols, stride)
        f[where, :] = f[where, :] - square[0:cols]
    out_ref[...] = f[pl.ds(pl.multiple_of(off, 8), rows), 0:cols]


def mirrored_sums(nz, b_vectors, gamma_density):
    nvec, rows, nmo = b_vectors.shape
    nocc = gamma_density.shape[2]
    cols = nocc // (nz * PAIR)
    hx = nocc // PAIR
    tiles = hx // SUB
    ta = min(tiles, (tiles // 2 + 6) // 7 * 7)
    tb = tiles - ta
    tz = pl.cdiv(cols, SUB)
    nch = pl.cdiv(rows, LANES)
    depth = nvec * rows
    vmem = pltpu.VMEM
    dma = pltpu.SemaphoreType.DMA
    flops = 2 * depth * nmo * nocc
    parts = [packed_tiles(n) for n in (PAIR * ta, PAIR * tb, tb, ta)]
    blocks = [vmem((nch, n, SUB, LANES), F32) for n in parts]
    return pl.pallas_call(
        functools.partial(kernel, nz, rows, cols, nmo // nocc, ta),
        out_shape=jax.ShapeDtypeStruct((rows, cols), F32),
        in_specs=[pl.BlockSpec(memory_space=pl.ANY), pl.BlockSpec(memory_space=pl.ANY)],
        out_specs=pl.BlockSpec(memory_space=vmem),
        scratch_shapes=[
            vmem((2 * PAIR, depth, PAIR * LANES), jnp.bfloat16),
            vmem((nvec, nocc, rows), jnp.bfloat16),
            vmem((nocc, depth), jnp.bfloat16),
            vmem((nch, PAIR, PAIR, tiles, SUB, LANES), F32),
            vmem((nch, PAIR, PAIR, tiles, SUB, LANES), F32),
            vmem((nch, PAIR, PAIR, tiles, SUB, LANES), F32),
            *blocks,
            *blocks,
            vmem((nch, tiles, SUB, LANES), F32),
            vmem((nch, 2, tz, SUB, LANES), F32),
            vmem((nch, 2, tz, SUB, LANES), F32),
            vmem((nch, tz, SUB, LANES), F32),
            vmem((nch * LANES, LANES), F32),
            vmem((2, tz * SUB, LANES), F32),
            vmem((2, tz * SUB, LANES), F32),
            dma((2 * PAIR, nvec * PAIR)),
            dma((nvec,)),
            dma((2, nch)),
            dma((2, nch)),
            dma((2, nch)),
            dma((2, nch)),
            dma((2, nch)),
            dma((2, nch, 2)),
            dma((2, nch)),
            dma((2, 2)),
        ],
        compiler_params=pltpu.CompilerParams(
            collective_id=0, has_side_effects=True, vmem_limit_bytes=60 * 2**20
        ),
        cost_estimate=pl.CostEstimate(flops=flops, bytes_accessed=2 * depth * nmo, transcendentals=0),
    )(b_vectors, jnp.transpose(gamma_density, (0, 2, 1)))


def solution(mesh):
    nchol, norb = mesh.shape["chol"], mesh.shape["orb"]

    def shards(b_vectors, gamma_density):
        nvec, rows, nmo = b_vectors.shape
        nocc = gamma_density.shape[2]
        cols = nocc // nchol
        fits = (
            norb == PAIR * PAIR
            and nchol == PAIR * norb
            and (PAIR * rows) % LANES == 0
            and rows % 16 == 0
            and nocc % (PAIR * nchol) == 0
            and (nocc // PAIR) % SUB == 0
            and nchol == 8
            and cols % SUB * (nchol // PAIR) <= SUB
            and (nvec * rows) % LANES == 0
            and nmo % nocc == 0
            and rows % (nmo // nocc) == 0
        )
        if fits:
            return mirrored_sums(nchol // PAIR, b_vectors, gamma_density)
        return gathered(b_vectors, gamma_density)

    in_specs = (P("chol", "orb", None), P("chol", "orb", None))
    out_specs = P("orb", "chol")
    return jax.shard_map(shards, mesh=mesh, in_specs=in_specs, out_specs=out_specs, check_vma=False)
```
